256 devices in a mesh: dec: 16 (over z, core), tp: 16 (over y, x).
Axes of the slice: x: 4, y: 4, z: 8, core: 2. Of those that a mesh axis runs over, the one named last changes fastest.
Arguments:
- hidden: float32 [16, 32, 4, 4096], P('dec', 'tp'), may hold values from -500 to 500
- norm_gain: float32 [4096], replicated, may hold values from 0.5 to 1.5
- lm_head: bfloat16 [131072, 4096], P(('dec', 'tp')), may hold values from -1 to 1
- token_ids: int32 [16, 32, 4], P('dec'), may hold values from 0 to 131071
- doc_counts: int32 [16], P('dec'), may hold values from 8 to 32, as said below
Outputs:
- hyp_score: float32 [16, 32], P('dec', 'tp')
- posterior: float32 [16, 32], P('dec', 'tp')
The draws below stay inside these ranges and needn't reach their ends.
Inputs may be any that keep to these rules, and one draw needn't show every extreme that they name: Document d's live hypotheses are its slots 0 to doc_counts[d] - 1; some document has 32.
All inputs are finite; a program needn't handle non-finite values.
Results may differ from the reference program's by a relative error of at most 0.0021.
Values may be sent and summed in bfloat16 or wider, within the bound.
No kernel may reach another device: no remote copies, remote signals or barrier semaphores. Data moves between devices by JAX's collectives and lax.ppermute only.
A program may use at most 64 MiB of HBM per device.

```python
import math
import jax
import jax.numpy as jnp
from jax import lax

D = 4096
LEN = 4
VOCAB = 131072
HYP_SLOT = 32
HYP_CAP = 32
DOCS = 16


def log_uniform(key, shape, low, high):
    return jnp.exp(jax.random.uniform(key, shape, jnp.float32, math.log(low), math.log(high)))


def draw_lm_head(key, part):
    row_scale = log_uniform(jax.random.fold_in(key, 1), (VOCAB, 1), 1.0, 10.0)
    entries = jnp.clip(jax.random.normal(jax.random.fold_in(key, 2), (VOCAB, D), jnp.float32), -5.0, 5.0)
    weights = entries * row_scale / D ** 0.5
    return weights.astype(jnp.bfloat16)


def draw_hidden(key, part):
    shape = (DOCS, HYP_SLOT, LEN, D)
    col_scale = log_uniform(jax.random.fold_in(key, 11), (D,), 1.0, 10.0)
    row_scale = log_uniform(jax.random.fold_in(key, 12), (DOCS, HYP_SLOT, LEN, 1), 1.0, 10.0)
    entries = jnp.clip(jax.random.normal(jax.random.fold_in(key, 14), shape, jnp.float32), -5.0, 5.0)
    values = entries * row_scale * col_scale
    return values


def draw_doc_counts(key, part):
    values = jax.random.randint(jax.random.fold_in(key, 21), (DOCS,), HYP_SLOT // 4, HYP_CAP + 1, jnp.int32)
    fullest = jax.random.randint(jax.random.fold_in(key, 22), (), 0, DOCS, jnp.int32)
    return values.at[fullest].set(HYP_CAP)


def set_ends(values, rng, low, top_value):
    place = [jax.random.randint(jax.random.fold_in(rng, axis), (), 0, length) for axis, length in enumerate(values.shape)]
    longest = values.shape.index(max(values.shape))
    beside = place[:longest] + [(place[longest] + 1) % values.shape[longest]] + place[longest + 1:]
    return values.at[tuple(place)].set(low).at[tuple(beside)].set(top_value)


def setup_inputs(seed: int = 0) -> dict:
    key_of = jax.random.split(jax.random.key(seed), 6)
    return {
        "hidden": draw_hidden(jax.random.fold_in(key_of[5], 71), 0),
        "norm_gain": jnp.clip(1.0 + 0.1 * jax.random.normal(key_of[1], (D,), jnp.float32), 0.5, 1.5),
        "lm_head": draw_lm_head(jax.random.fold_in(key_of[5], 71), 0),
        "token_ids": set_ends(jax.random.randint(key_of[3], (DOCS, HYP_SLOT, LEN), 0, VOCAB), jax.random.fold_in(key_of[3], 1), 0, VOCAB - 1).astype(jnp.int32),
        "doc_counts": draw_doc_counts(jax.random.fold_in(key_of[5], 71), 0),
    }


def reference(hidden, norm_gain, lm_head, token_ids, doc_counts):
    flat = hidden.reshape(-1, D)
    meansq = lax.optimization_barrier(jnp.mean(flat * flat, axis=1, keepdims=True))
    normed = (flat * lax.rsqrt(meansq + 1e-05) * norm_gain).astype(jnp.bfloat16)
    flat_ids = token_ids.reshape(-1).astype(jnp.int32)
    total_rows = flat.shape[0]
    block_size = math.gcd(total_rows, 256)

    def score_block(inputs):
        block_rows, block_ids = inputs
        logits = lax.dot_general(block_rows, lm_head, (((1,), (1,)), ((), ())), preferred_element_type=jnp.float32)
        log_total = jax.nn.logsumexp(logits, axis=1)
        target = jnp.take_along_axis(logits, block_ids[:, None], axis=1)[:, 0]
        return target - log_total
    token_logp = lax.map(score_block, (normed.reshape(-1, block_size, D), flat_ids.reshape(-1, block_size)))
    token_logp = token_logp.reshape(DOCS, HYP_SLOT, LEN)
    score = lax.optimization_barrier(jnp.sum(token_logp, axis=2)) / LEN
    slot_ids = jnp.arange(HYP_SLOT, dtype=jnp.int32)
    alive = slot_ids[None, :] < doc_counts[:, None]
    best_score = lax.optimization_barrier(jnp.max(jnp.where(alive, score, -jnp.inf), axis=1, keepdims=True))
    doc_norm = best_score + jnp.log(lax.optimization_barrier(jnp.sum(jnp.exp(jnp.where(alive, score - best_score, -jnp.inf)), axis=1, keepdims=True)))
    hyp_score = jnp.where(alive, score, 0.0)
    posterior = jnp.where(alive, score - doc_norm, 0.0)
    return (hyp_score, posterior)
```

```python
import jax
import jax.numpy as jnp
from jax import lax
from jax.sharding import Mesh, PartitionSpec as P


def rms_normed(hidden, norm_gain):
    flat = hidden.reshape(-1, hidden.shape[-1])
    meansq = jnp.mean(flat * flat, axis=1, keepdims=True)
    return (flat * lax.rsqrt(meansq + 1e-05) * norm_gain).astype(jnp.bfloat16)


def spread(block, axis):
    count = lax.axis_size(axis)
    return lax.all_to_all(
        jnp.broadcast_to(block[None], (count,) + block.shape), axis, 0, 0, tiled=True
    )


def shifted(block, axis, step):
    count = lax.axis_size(axis)
    return lax.ppermute(block, axis, [(i, (i + step) % count) for i in range(count)])


def joined(parts, axis):
    count = len(parts)
    index = lax.axis_index(axis)
    stacked = jnp.stack(parts[::-1])
    return jnp.roll(stacked, index + 1, axis=0)


def merge_logs(logs):
    peak = jnp.max(logs, axis=0)
    return peak + jnp.log(jnp.sum(jnp.exp(logs - peak[None]), axis=0))


def body(hidden, norm_gain, lm_head, token_ids, doc_counts):
    z, c, y, x = (lax.axis_index(a) for a in "zcyx")
    nz, nc, ny, nx = (lax.axis_size(a) for a in "zcyx")
    tp_count = ny * nx
    tp_index = y * nx + x
    slots, length = hidden.shape[1], hidden.shape[2]
    rows = slots * length
    vocab_rows, width = lm_head.shape
    tokens = tp_count * rows

    other_head = shifted(lm_head, "c", 1)
    normed = rms_normed(hidden, norm_gain)
    ids = token_ids.reshape(-1)
    digits = jnp.stack([ids // 65536, (ids // 256) % 256, ids % 256])
    digits = jnp.pad(digits, ((0, rows - 3), (0, 0))).astype(jnp.bfloat16)
    planes = spread(jnp.concatenate([normed, digits], axis=1), "z")
    got = planes[:, :3, width:].astype(jnp.int32)
    all_ids = got[:, 0] * 65536 + got[:, 1] * 256 + got[:, 2]

    half = nz // 2
    block_a = spread(planes[:half, :, :width], "y")
    block_b = spread(planes[half:, :, :width], "x")
    parts_a = [block_a] + [shifted(block_a, "x", k) for k in range(1, nx)]
    parts_b = [block_b] + [shifted(block_b, "y", k) for k in range(1, ny)]

    heads = (lm_head, other_head)
    starts = [((z * nc + core) * tp_count + tp_index) * vocab_rows for core in (c, nc - 1 - c)]
    ids_grid = all_ids.reshape(nz, ny, nx, rows)
    vocab = jnp.arange(vocab_rows, dtype=jnp.int32)

    def stats(block, block_ids):
        flat = block.reshape(-1, width)
        flat_ids = block_ids.reshape(-1)
        logits = [
            lax.dot_general(flat, head, (((1,), (1,)), ((), ())), preferred_element_type=jnp.float32)
            for head in heads
        ]
        peak = jnp.maximum(jnp.max(logits[0], axis=1), jnp.max(logits[1], axis=1))
        total = sum(jnp.sum(jnp.exp(part - peak[:, None]), axis=1) for part in logits)
        target = sum(
            jnp.sum(jnp.where(vocab[None, :] == (flat_ids - start)[:, None], part, 0.0), axis=1)
            for part, start in zip(logits, starts)
        )
        return jnp.stack([peak + jnp.log(total), target])

    def pick(grid, axis, index, step, count):
        return jnp.take(grid, (index - step + count) % count, axis=axis)

    out_a = [
        stats(part, pick(ids_grid[:half], 2, x, k, nx).transpose(1, 0, 2))
        for k, part in enumerate(parts_a)
    ]
    out_b = [
        stats(part, pick(ids_grid[half:], 1, y, k, ny).transpose(1, 0, 2))
        for k, part in enumerate(parts_b)
    ]
    stats_a = joined(out_a, "x").reshape(nx, 2, ny, half, rows).transpose(3, 1, 2, 0, 4)
    stats_b = joined(out_b, "y").reshape(ny, 2, nx, half, rows).transpose(3, 1, 0, 2, 4)
    sent = jnp.concatenate([stats_a, stats_b]).reshape(nz, 2, tokens)
    mine = lax.all_to_all(sent, "z", 0, 0, tiled=True)
    partial = jnp.stack([merge_logs(mine[:, 0]), jnp.sum(mine[:, 1], axis=0)])
    whole = spread(partial, ("y", "x"))
    token_logp = jnp.sum(whole[:, 1], axis=0) - merge_logs(whole[:, 0])
    scores = jnp.sum(token_logp.reshape(-1, length), axis=1) / length
    alive = jnp.arange(scores.shape[0], dtype=jnp.int32) < doc_counts[0]
    best = jnp.max(jnp.where(alive, scores, -jnp.inf))
    doc_norm = best + jnp.log(jnp.sum(jnp.exp(jnp.where(alive, scores - best, -jnp.inf))))
    hyp_score = jnp.where(alive, scores, 0.0)
    posterior = jnp.where(alive, scores - doc_norm, 0.0)
    own = tp_index * slots
    return tuple(lax.dynamic_slice_in_dim(v, own, slots)[None, :] for v in (hyp_score, posterior))


def solution(mesh):
    cores = 2
    side = 4
    dec, tp = mesh.devices.shape
    fine = Mesh(mesh.devices.reshape(dec // cores, cores, tp // side, side), ("z", "c", "y", "x"))
    docs, slots = ("z", "c"), ("y", "x")
    return jax.shard_map(
        body,
        mesh=fine,
        in_specs=(
            P(docs, slots, None, None),
            P(),
            P(("z", "c", "y", "x"), None),
            P(docs, None, None),
            P(docs),
        ),
        out_specs=(P(docs, slots), P(docs, slots)),
        check_vma=False,
    )
```

```python
import functools

import jax
import jax.numpy as jnp
from jax import lax
from jax.experimental import pallas as pl
from jax.experimental.pallas import tpu as pltpu
from jax.sharding import Mesh, PartitionSpec as P


LANES = 128
NZ, NC, NY, NX = 8, 2, 4, 4
TP = NY * NX
HALF = NZ // 2
VMEM = pltpu.VMEM
SMEM = pltpu.SMEM
NT = (((1,), (1,)), ((), ()))


def norm_kernel(ids_ref, hidden_ref, gain_ref, out_ref, work):
    slots, length, width = hidden_ref.shape[1:]
    rows = slots * length
    for slot in range(slots):
        work[pl.ds(slot * length, length), :] = hidden_ref[0, slot]
    flat = work[...]
    meansq = jnp.mean(flat * flat, axis=1, keepdims=True)
    normed = (flat * lax.rsqrt(meansq + 1e-05) * gain_ref[...]).astype(jnp.bfloat16)
    first = (lax.axis_index("y") * NX + lax.axis_index("x")) * rows
    row = lax.broadcasted_iota(jnp.int32, (rows, LANES), 0)
    lane = lax.broadcasted_iota(jnp.int32, (rows, LANES), 1)
    ids = jnp.zeros((rows, LANES), jnp.int32)
    for r in range(rows):
        ids = jnp.where(row == r, ids_ref[first + r], ids)
    digit = jnp.where(lane == 0, ids >> 16, jnp.where(lane == 1, (ids >> 8) & 255, ids & 255))
    digit = jnp.where(lane < 3, digit, 0).astype(jnp.float32).astype(jnp.bfloat16)
    for copy in range(out_ref.shape[0]):
        out_ref[copy, :, :width] = normed
        out_ref[copy, :, width:] = digit


def norm_rows(hidden, norm_gain, token_ids):
    slots, length, width = hidden.shape[1:]
    rows = slots * length
    return pl.pallas_call(
        norm_kernel,
        out_shape=jax.ShapeDtypeStruct((NZ, rows, width + LANES), jnp.bfloat16),
        in_specs=[
            pl.BlockSpec(memory_space=SMEM),
            pl.BlockSpec(memory_space=VMEM),
            pl.BlockSpec(memory_space=VMEM),
        ],
        out_specs=pl.BlockSpec(memory_space=VMEM),
        scratch_shapes=[VMEM((rows, width), jnp.float32)],
        name="norm_rows",
    )(token_ids.reshape(-1), hidden, norm_gain.reshape(1, -1))


def by_plane(value):
    lane = lax.broadcasted_iota(jnp.int32, value.shape, 1)
    shift = lane // 32 - lane % 32 // 8
    out = value
    for d in (-3, -2, -1, 1, 2, 3):
        out = jnp.where(shift == d, pltpu.roll(value, 24 * d % LANES, 1), out)
    return out


def score_kernel(parts, steps, earlier, *refs):
    rows = refs[:parts]
    digits = refs[parts : 2 * parts]
    heads = refs[2 * parts : 2 * parts + 2]
    before = refs[2 * parts + 2 : 2 * parts + 2 + earlier]
    out_ref, acc = refs[2 * parts + 2 + earlier :]
    step = pl.program_id(0)
    vocab = heads[0].shape[0]
    block = jnp.concatenate([r[...] for r in rows], axis=0)
    for i, head in enumerate(heads):
        part = lax.dot_general(head[...], block, NT, preferred_element_type=jnp.float32)
        span = pl.ds(i * vocab, vocab)

        @pl.when(step == 0)
        def _():
            acc[span, :] = part

        @pl.when(step > 0)
        def _():
            acc[span, :] += part

    @pl.when(step == steps - 1)
    def _():
        tokens = acc.shape[1]
        columns = jnp.concatenate([d[...] for d in digits], axis=0)
        lane = lax.broadcasted_iota(jnp.int32, (8, LANES), 1)
        weight = jnp.where(lane == 0, 65536.0, jnp.where(lane == 1, 256.0, jnp.where(lane == 2, 1.0, 0.0)))
        ids = lax.dot_general(weight.astype(jnp.bfloat16), columns, NT, preferred_element_type=jnp.float32)
        ids = ids[0:1].astype(jnp.int32)
        z, c = lax.axis_index("z"), lax.axis_index("c")
        place = lax.axis_index("y") * NX + lax.axis_index("x")
        peak = jnp.max(acc[...], axis=0, keepdims=True)
        total = jnp.zeros((1, tokens), jnp.float32)
        target = jnp.zeros((1, tokens), jnp.float32)
        for i in range(2):
            core = c if i == 0 else NC - 1 - c
            local = ids - ((z * NC + core) * TP + place) * vocab
            logits = acc[pl.ds(i * vocab, vocab), :]
            total += jnp.sum(jnp.exp(logits - peak), axis=0, keepdims=True)
            entry = lax.broadcasted_iota(jnp.int32, (vocab, tokens), 0)
            target += jnp.sum(jnp.where(entry == local, logits, 0.0), axis=0, keepdims=True)
        stats = jnp.concatenate([peak + jnp.log(total), target], axis=0)
        stats = jnp.concatenate([by_plane(stats[:, :LANES]), by_plane(stats[:, LANES:])], axis=1)
        if not earlier:
            out_ref[...] = stats
        else:
            groups = [b[...] for b in before] + [stats]
            lanes = lax.broadcasted_iota(jnp.int32, (2, LANES), 1) // (LANES // 4)
            order = (0, 1, 3, 2)
            for zz in range(NZ):
                side = pl.ds((zz // HALF) * LANES, LANES)
                value = jnp.zeros((2, LANES), jnp.float32)
                for k, group in zip(order, groups):
                    half = group[:, (zz // HALF) * LANES : (zz // HALF + 1) * LANES]
                    turn = ((k - zz % HALF) * (LANES // 4)) % LANES
                    moved = pltpu.roll(half, turn, 1) if turn else half
                    value = jnp.where(lanes == k, moved, value)
                out_ref[zz] = value


def score_group(parts, heads, earlier=()):
    vocab, width = heads[0].shape
    steps = 4
    depth = width // steps
    tokens = sum(p.shape[0] for p in parts)
    shape = (NZ, 2, LANES) if earlier else (2, tokens)
    specs = [pl.BlockSpec((p.shape[0], depth), lambda k: (0, k)) for p in parts]
    specs += [pl.BlockSpec((p.shape[0], LANES), lambda k: (0, width // LANES)) for p in parts]
    specs += [pl.BlockSpec((vocab, depth), lambda k: (0, k)) for _ in heads]
    specs += [pl.BlockSpec(e.shape, lambda k: (0, 0)) for e in earlier]
    return pl.pallas_call(
        functools.partial(score_kernel, len(parts), steps, len(earlier)),
        out_shape=jax.ShapeDtypeStruct(shape, jnp.float32),
        grid_spec=pltpu.PrefetchScalarGridSpec(
            num_scalar_prefetch=0,
            grid=(steps,),
            in_specs=specs,
            out_specs=pl.BlockSpec(shape, lambda k: (0,) * len(shape)),
            scratch_shapes=[VMEM((2 * vocab, tokens), jnp.float32)],
        ),
        cost_estimate=pl.CostEstimate(
            flops=4 * vocab * tokens * width,
            bytes_accessed=(2 * vocab + tokens) * width * 2,
            transcendentals=2 * vocab * tokens,
        ),
        name="score_group",
    )(*parts, *parts, *heads, *earlier)


def merged(ref):
    count = ref.shape[0]
    peak = ref[0, 0:1]
    for i in range(1, count):
        peak = jnp.maximum(peak, ref[i, 0:1])
    total = jnp.exp(ref[0, 0:1] - peak)
    target = ref[0, 1:2]
    for i in range(1, count):
        total += jnp.exp(ref[i, 0:1] - peak)
        target += ref[i, 1:2]
    return peak + jnp.log(total), target


def merge_kernel(in_ref, out_ref):
    log_total, target = merged(in_ref)
    value = jnp.concatenate([log_total, target], axis=0)
    first = lax.axis_index("z") < HALF
    y, x = lax.axis_index("y"), lax.axis_index("x")
    outer = jnp.where(first, x, y)
    inner = jnp.where(first, y, x)
    lane = lax.broadcasted_iota(jnp.int32, value.shape, 1) % 32
    value = pltpu.roll(value, outer * 32, 1)
    value = jnp.where(
        lane >= inner * 8,
        pltpu.roll(value, inner * 8, 1),
        pltpu.roll(value, lax.rem(inner * 8 + 96, 128), 1),
    )
    for i in range(out_ref.shape[0]):
        out_ref[i] = value


def merge_docs(mine):
    return pl.pallas_call(
        merge_kernel,
        out_shape=jax.ShapeDtypeStruct((TP, 2, LANES), jnp.float32),
        in_specs=[pl.BlockSpec(memory_space=VMEM)],
        out_specs=pl.BlockSpec(memory_space=VMEM),
        name="merge_docs",
    )(mine)


def final_kernel(length, slots, counts_ref, in_ref, hyp_ref, post_ref):
    log_total, target = merged(in_ref)
    logp = target - log_total
    score = logp
    for k in range(1, length):
        score = score + pltpu.roll(logp, LANES - k, 1)
    score = score / length
    first = lax.axis_index("z") < HALF
    y, x = lax.axis_index("y"), lax.axis_index("x")
    lane = lax.broadcasted_iota(jnp.int32, score.shape, 1)
    outer, inner, row = lane // 32, lane % 32 // 8, lane % 8
    place = jnp.where(first, inner * NX + outer, outer * NX + inner)
    slot = place * slots + row // length
    head = row % length == 0
    alive = slot < counts_ref[0]
    live = jnp.logical_and(head, alive)
    best = jnp.max(jnp.where(live, score, -jnp.inf), axis=1, keepdims=True)
    total = jnp.sum(jnp.where(live, jnp.exp(jnp.where(live, score - best, 0.0)), 0.0), axis=1, keepdims=True)
    doc_norm = best + jnp.log(total)
    own = jnp.where(first, x * 32 + y * 8, y * 32 + x * 8)
    turn = lax.rem(LANES - own, LANES)
    for value, ref in ((score, hyp_ref), (score - doc_norm, post_ref)):
        value = jnp.where(alive, value, 0.0)
        value = pltpu.roll(value, turn, 1)
        value = jnp.where(lane == 0, value, pltpu.roll(value, LANES - length + 1, 1))
        ref[...] = value[:, :slots]


def final_scores(whole, doc_counts, length, slots):
    out = jax.ShapeDtypeStruct((1, slots), jnp.float32)
    return pl.pallas_call(
        functools.partial(final_kernel, length, slots),
        out_shape=(out, out),
        in_specs=[pl.BlockSpec(memory_space=SMEM), pl.BlockSpec(memory_space=VMEM)],
        out_specs=(pl.BlockSpec(memory_space=VMEM), pl.BlockSpec(memory_space=VMEM)),
        name="final_scores",
    )(doc_counts, whole)


def fetched(block, axis, step):
    count = lax.axis_size(axis)
    return lax.ppermute(block, axis, [((i + step) % count, i) for i in range(count)])


def body(hidden, norm_gain, lm_head, token_ids, doc_counts):
    slots, length = hidden.shape[1], hidden.shape[2]
    payload = norm_rows(hidden, norm_gain, token_ids)
    planes = lax.all_to_all(payload, "z", 0, 0, tiled=True)
    planes, other = lax.optimization_barrier((planes, fetched(lm_head, "c", 1)))
    heads = (lm_head, other)
    wide = planes.shape[-1]

    def gathered(block, axis):
        return jnp.stack([block] + [fetched(block, axis, k) for k in range(1, 4)])

    block_a = gathered(planes[:HALF], "y")
    block_b = gathered(planes[HALF:], "x")

    def flat(*blocks):
        return tuple(b.reshape(-1, wide) for b in blocks)

    near = (
        fetched(block_a, "x", 1),
        fetched(block_b, "y", 1),
        fetched(block_a, "x", 3),
        fetched(block_b, "y", 3),
    )
    first = score_group(flat(block_a, block_b), heads)
    near, first = lax.optimization_barrier((near, first))
    after_a, after_b, before_a, before_b = near
    far_a = fetched(after_a[:2], "x", 1), fetched(before_a[2:], "x", 3)
    far_b = fetched(after_b[:2], "y", 1), fetched(before_b[2:], "y", 3)
    second = score_group(flat(after_a, after_b), heads)
    third = score_group(flat(before_a, before_b), heads)
    sent = score_group(flat(*far_a, *far_b), heads, (first, second, third))
    mine = lax.all_to_all(sent, "z", 0, 0, tiled=True)
    whole = lax.all_to_all(merge_docs(mine), ("y", "x"), 0, 0, tiled=True)
    return final_scores(whole, doc_counts, length, slots)


def solution(mesh):
    fine = Mesh(mesh.devices.reshape(NZ, NC, NY, NX), ("z", "c", "y", "x"))
    docs, slots = ("z", "c"), ("y", "x")
    return jax.shard_map(
        body,
        mesh=fine,
        in_specs=(
            P(docs, slots, None, None),
            P(),
            P(("z", "c", "y", "x"), None),
            P(docs, None, None),
            P(docs),
        ),
        out_specs=(P(docs, slots), P(docs, slots)),
        check_vma=False,
    )
```

```python
import functools

import jax
import jax.numpy as jnp
from jax import lax
from jax.experimental import pallas as pl
from jax.experimental.pallas import tpu as pltpu
from jax.sharding import Mesh, PartitionSpec as P


LANES = 128
NZ, NC, NY, NX = 8, 2, 4, 4
TP = NY * NX
HALF = NZ // 2
VMEM = pltpu.VMEM
SMEM = pltpu.SMEM
PARAMS = pltpu.CompilerParams(vmem_limit_bytes=16 * 2**20)
NT = (((1,), (1,)), ((), ()))


def norm_kernel(ids_ref, hidden_ref, gain_ref, out_ref, work, id_work):
    slots, length, width = hidden_ref.shape[1:]
    rows = slots * length
    place = lax.axis_index("y") * NX + lax.axis_index("x")
    ids = ids_ref[0].astype(jnp.float32)
    slot_lane = lax.broadcasted_iota(jnp.int32, ids.shape, 1)
    for slot in range(slots):
        span = pl.ds(slot * length, length)
        work[span, :] = hidden_ref[0, slot]
        own = jnp.sum(jnp.where(slot_lane == place * slots + slot, ids, 0.0), axis=1, keepdims=True)
        id_work[span, :] = jnp.broadcast_to(own, (length, LANES))
    flat = work[...]
    meansq = jnp.mean(flat * flat, axis=1, keepdims=True)
    normed = (flat * lax.rsqrt(meansq + 1e-05) * gain_ref[...]).astype(jnp.bfloat16)
    lane = lax.broadcasted_iota(jnp.int32, (rows, LANES), 1)
    value = id_work[...].astype(jnp.int32)
    digit = jnp.where(lane == 0, value >> 16, jnp.where(lane == 1, (value >> 8) & 255, value & 255))
    digit = jnp.where(lane < 3, digit, 0).astype(jnp.float32).astype(jnp.bfloat16)
    for copy in range(out_ref.shape[0]):
        out_ref[copy, :, :width] = normed
        out_ref[copy, :, width:] = digit


def norm_rows(hidden, norm_gain, token_ids):
    slots, length, width = hidden.shape[1:]
    rows = slots * length
    return pl.pallas_call(
        norm_kernel,
        out_shape=jax.ShapeDtypeStruct((NZ, rows, width + LANES), jnp.bfloat16),
        in_specs=[pl.BlockSpec(memory_space=VMEM)] * 3,
        out_specs=pl.BlockSpec(memory_space=VMEM),
        scratch_shapes=[VMEM((rows, width), jnp.float32), VMEM((rows, LANES), jnp.float32)],
        compiler_params=PARAMS,
        name="norm_rows",
    )(token_ids.transpose(0, 2, 1), hidden, norm_gain.reshape(1, -1))


def by_plane(value):
    lane = lax.broadcasted_iota(jnp.int32, value.shape, 1)
    shift = lane // 32 - lane % 32 // 8
    out = value
    for d in (-3, -2, -1, 1, 2, 3):
        out = jnp.where(shift == d, pltpu.roll(value, 24 * d % LANES, 1), out)
    return out


def score_kernel(parts, earlier, *refs):
    rows, heads = refs[:parts], refs[parts : parts + 2]
    before = refs[parts + 2 : parts + 2 + earlier]
    out_ref, acc = refs[parts + 2 + earlier :]
    vocab, width = heads[0].shape
    tokens = acc.shape[1]
    block = jnp.concatenate([r[:, :width] for r in rows], axis=0)
    for i, head in enumerate(heads):
        acc[pl.ds(i * vocab, vocab), :] = lax.dot_general(
            head[...], block, NT, preferred_element_type=jnp.float32
        )
    columns = jnp.concatenate([r[:, width:] for r in rows], axis=0)
    lane = lax.broadcasted_iota(jnp.int32, (8, LANES), 1)
    weight = jnp.where(lane == 0, 65536.0, jnp.where(lane == 1, 256.0, jnp.where(lane == 2, 1.0, 0.0)))
    ids = lax.dot_general(weight.astype(jnp.bfloat16), columns, NT, preferred_element_type=jnp.float32)
    ids = ids[0:1].astype(jnp.int32)
    z, c = lax.axis_index("z"), lax.axis_index("c")
    place = lax.axis_index("y") * NX + lax.axis_index("x")
    peak = jnp.max(acc[...], axis=0, keepdims=True)
    total = jnp.zeros((1, tokens), jnp.float32)
    target = jnp.zeros((1, tokens), jnp.float32)
    chunk = LANES
    for i in range(2):
        core = c if i == 0 else NC - 1 - c
        local = ids - ((z * NC + core) * TP + place) * vocab

        def add(j, sums):
            logits = acc[pl.ds(pl.multiple_of(i * vocab + j * chunk, chunk), chunk), :]
            entry = lax.broadcasted_iota(jnp.int32, logits.shape, 0) + j * chunk
            return (
                sums[0] + jnp.sum(jnp.exp(logits - peak), axis=0, keepdims=True),
                sums[1] + jnp.sum(jnp.where(entry == local, logits, 0.0), axis=0, keepdims=True),
            )

        total, target = lax.fori_loop(0, vocab // chunk, add, (total, target))
    stats = jnp.concatenate([peak + jnp.log(total), target], axis=0)
    stats = jnp.concatenate([by_plane(stats[:, :LANES]), by_plane(stats[:, LANES:])], axis=1)
    if not earlier:
        out_ref[...] = stats
    else:
        groups = [b[...] for b in before] + [stats]
        lanes = lax.broadcasted_iota(jnp.int32, (2, LANES), 1) // (LANES // 4)
        order = (0, 1, 3, 2)
        for zz in range(NZ):
            value = jnp.zeros((2, LANES), jnp.float32)
            for k, group in zip(order, groups):
                half = group[:, (zz // HALF) * LANES : (zz // HALF + 1) * LANES]
                turn = ((k - zz % HALF) * (LANES // 4)) % LANES
                moved = pltpu.roll(half, turn, 1) if turn else half
                value = jnp.where(lanes == k, moved, value)
            out_ref[zz] = value


def in_vmem(array):
    return pltpu.with_memory_space_constraint(array, VMEM)


def score_group(parts, heads, earlier=()):
    vocab, width = heads[0].shape
    tokens = sum(p.shape[0] for p in parts)
    shape = (NZ, 2, LANES) if earlier else (2, tokens)
    operands = [*map(in_vmem, parts), *heads, *earlier]
    return pl.pallas_call(
        functools.partial(score_kernel, len(parts), len(earlier)),
        out_shape=jax.ShapeDtypeStruct(shape, jnp.float32),
        in_specs=[pl.BlockSpec(memory_space=VMEM)] * len(operands),
        out_specs=pl.BlockSpec(memory_space=VMEM),
        scratch_shapes=[VMEM((2 * vocab, tokens), jnp.float32)],
        compiler_params=PARAMS,
        cost_estimate=pl.CostEstimate(
            flops=4 * vocab * tokens * width,
            bytes_accessed=(2 * vocab + tokens) * width * 2,
            transcendentals=2 * vocab * tokens,
        ),
        name="score_group",
    )(*operands)


def merged(ref):
    count = ref.shape[0]
    peak = ref[0, 0:1]
    for i in range(1, count):
        peak = jnp.maximum(peak, ref[i, 0:1])
    total = jnp.exp(ref[0, 0:1] - peak)
    target = ref[0, 1:2]
    for i in range(1, count):
        total += jnp.exp(ref[i, 0:1] - peak)
        target += ref[i, 1:2]
    return peak + jnp.log(total), target


def merge_kernel(in_ref, out_ref):
    log_total, target = merged(in_ref)
    value = jnp.concatenate([log_total, target], axis=0)
    first = lax.axis_index("z") < HALF
    y, x = lax.axis_index("y"), lax.axis_index("x")
    outer = jnp.where(first, x, y)
    inner = jnp.where(first, y, x)
    lane = lax.broadcasted_iota(jnp.int32, value.shape, 1) % 32
    value = pltpu.roll(value, outer * 32, 1)
    value = jnp.where(
        lane >= inner * 8,
        pltpu.roll(value, inner * 8, 1),
        pltpu.roll(value, lax.rem(inner * 8 + 96, 128), 1),
    )
    for i in range(out_ref.shape[0]):
        out_ref[i] = value


def merge_docs(mine):
    return pl.pallas_call(
        merge_kernel,
        out_shape=jax.ShapeDtypeStruct((TP, 2, LANES), jnp.float32),
        in_specs=[pl.BlockSpec(memory_space=VMEM)],
        out_specs=pl.BlockSpec(memory_space=VMEM),
        compiler_params=PARAMS,
        name="merge_docs",
    )(in_vmem(mine))


def final_kernel(length, slots, counts_ref, in_ref, hyp_ref, post_ref):
    log_total, target = merged(in_ref)
    logp = target - log_total
    score = logp
    for k in range(1, length):
        score = score + pltpu.roll(logp, LANES - k, 1)
    score = score / length
    first = lax.axis_index("z") < HALF
    y, x = lax.axis_index("y"), lax.axis_index("x")
    lane = lax.broadcasted_iota(jnp.int32, score.shape, 1)
    outer, inner, row = lane // 32, lane % 32 // 8, lane % 8
    place = jnp.where(first, inner * NX + outer, outer * NX + inner)
    slot = place * slots + row // length
    head = row % length == 0
    alive = slot < counts_ref[0]
    live = jnp.logical_and(head, alive)
    best = jnp.max(jnp.where(live, score, -jnp.inf), axis=1, keepdims=True)
    total = jnp.sum(jnp.where(live, jnp.exp(jnp.where(live, score - best, 0.0)), 0.0), axis=1, keepdims=True)
    doc_norm = best + jnp.log(total)
    own = jnp.where(first, x * 32 + y * 8, y * 32 + x * 8)
    turn = lax.rem(LANES - own, LANES)
    for value, ref in ((score, hyp_ref), (score - doc_norm, post_ref)):
        value = jnp.where(alive, value, 0.0)
        value = pltpu.roll(value, turn, 1)
        value = jnp.where(lane == 0, value, pltpu.roll(value, LANES - length + 1, 1))
        ref[...] = value[:, :slots]


def final_scores(whole, doc_counts, length, slots):
    out = jax.ShapeDtypeStruct((1, slots), jnp.float32)
    return pl.pallas_call(
        functools.partial(final_kernel, length, slots),
        out_shape=(out, out),
        in_specs=[pl.BlockSpec(memory_space=SMEM), pl.BlockSpec(memory_space=VMEM)],
        out_specs=(pl.BlockSpec(memory_space=VMEM), pl.BlockSpec(memory_space=VMEM)),
        compiler_params=PARAMS,
        name="final_scores",
    )(doc_counts, in_vmem(whole))


def fetched(block, axis, step):
    count = lax.axis_size(axis)
    return lax.ppermute(block, axis, [((i + step) % count, i) for i in range(count)])


def body(hidden, norm_gain, lm_head, token_ids, doc_counts):
    slots, length = hidden.shape[1], hidden.shape[2]
    payload = norm_rows(hidden, norm_gain, token_ids)
    planes = lax.all_to_all(payload, "z", 0, 0, tiled=True)
    planes, other = lax.optimization_barrier((planes, fetched(lm_head, "c", 1)))
    heads = (in_vmem(lm_head), in_vmem(other))
    wide = planes.shape[-1]

    def gathered(block, axis):
        pieces = [block] + [fetched(block, axis, k) for k in range(1, 4)]
        return jnp.stack(pieces[:2]), jnp.stack(pieces[2:])

    low_a, high_a = gathered(planes[:HALF], "y")
    low_b, high_b = gathered(planes[HALF:], "x")

    def flat(*blocks):
        return tuple(b.reshape(-1, wide) for b in blocks)

    relayed = (fetched(low_a, "x", 1), fetched(low_b, "y", 1), fetched(high_a, "x", 3), fetched(high_b, "y", 3))
    kept = (fetched(high_a, "x", 1), fetched(high_b, "y", 1), fetched(low_a, "x", 3), fetched(low_b, "y", 3))
    first = score_group(flat(low_a, high_a, low_b, high_b), heads)
    relayed, first = lax.optimization_barrier((relayed, first))
    far = (
        fetched(relayed[0], "x", 1),
        fetched(relayed[2], "x", 3),
        fetched(relayed[1], "y", 1),
        fetched(relayed[3], "y", 3),
    )
    second = score_group(flat(relayed[0], kept[0], relayed[1], kept[1]), heads)
    third = score_group(flat(kept[2], relayed[2], kept[3], relayed[3]), heads)
    sent = score_group(flat(*far), heads, (first, second, third))
    mine = lax.all_to_all(sent, "z", 0, 0, tiled=True)
    whole = lax.all_to_all(merge_docs(mine), ("y", "x"), 0, 0, tiled=True)
    return final_scores(whole, doc_counts, length, slots)


def solution(mesh):
    fine = Mesh(mesh.devices.reshape(NZ, NC, NY, NX), ("z", "c", "y", "x"))
    docs, slots = ("z", "c"), ("y", "x")
    return jax.shard_map(
        body,
        mesh=fine,
        in_specs=(
            P(docs, slots, None, None),
            P(),
            P(("z", "c", "y", "x"), None),
            P(docs, None, None),
            P(docs),
        ),
        out_specs=(P(docs, slots), P(docs, slots)),
        check_vma=False,
    )
```

```python
import functools

import jax
import jax.numpy as jnp
from jax import lax
from jax.experimental import pallas as pl
from jax.experimental.pallas import tpu as pltpu
from jax.sharding import Mesh, PartitionSpec as P


LANES = 128
NZ, NC, NY, NX = 8, 2, 4, 4
TP = NY * NX
DOCS_A, DOCS_B = (2, 3, 4), (5, 6)
VMEM = pltpu.VMEM
SMEM = pltpu.SMEM
PARAMS = pltpu.CompilerParams(vmem_limit_bytes=16 * 2**20)
NT = (((1,), (1,)), ((), ()))


def norm_kernel(ids_hbm, hidden_hbm, gain_hbm, out_ref, ids_ref, hidden_ref, gain_ref, work, id_work, sems):
    moves = ((hidden_hbm, hidden_ref), (gain_hbm, gain_ref), (ids_hbm, ids_ref))
    copies = [pltpu.make_async_copy(src, dst, sems.at[i]) for i, (src, dst) in enumerate(moves)]
    for copy in copies:
        copy.start()
    for copy in copies:
        copy.wait()
    slots, length, width = hidden_ref.shape[1:]
    rows = slots * length
    place = lax.axis_index("y") * NX + lax.axis_index("x")
    ids = ids_ref[0].astype(jnp.float32)
    slot_lane = lax.broadcasted_iota(jnp.int32, ids.shape, 1)
    for slot in range(slots):
        span = pl.ds(slot * length, length)
        work[span, :] = hidden_ref[0, slot]
        own = jnp.sum(jnp.where(slot_lane == place * slots + slot, ids, 0.0), axis=1, keepdims=True)
        id_work[span, :] = jnp.broadcast_to(own, (length, LANES))
    flat = work[...]
    meansq = jnp.mean(flat * flat, axis=1, keepdims=True)
    out_ref[:, :width] = (flat * lax.rsqrt(meansq + 1e-05) * gain_ref[...]).astype(jnp.bfloat16)
    lane = lax.broadcasted_iota(jnp.int32, (rows, LANES), 1)
    value = id_work[...].astype(jnp.int32)
    digit = jnp.where(lane == 0, value >> 16, jnp.where(lane == 1, (value >> 8) & 255, value & 255))
    out_ref[:, width:] = jnp.where(lane < 3, digit, 0).astype(jnp.float32).astype(jnp.bfloat16)


def norm_rows(hidden, norm_gain, token_ids):
    slots, length, width = hidden.shape[1:]
    rows = slots * length
    operands = (token_ids.transpose(0, 2, 1), hidden, norm_gain.reshape(1, -1))
    return pl.pallas_call(
        norm_kernel,
        out_shape=jax.ShapeDtypeStruct((rows, width + LANES), jnp.bfloat16),
        in_specs=[pl.BlockSpec(memory_space=pltpu.HBM)] * 3,
        out_specs=pl.BlockSpec(memory_space=VMEM),
        scratch_shapes=[VMEM(o.shape, o.dtype) for o in operands]
        + [
            VMEM((rows, width), jnp.float32),
            VMEM((rows, LANES), jnp.float32),
            pltpu.SemaphoreType.DMA((3,)),
        ],
        compiler_params=PARAMS,
        name="norm_rows",
    )(*(pltpu.with_memory_space_constraint(o, pltpu.HBM) for o in operands))


def score_kernel(pads, earlier, *refs):
    parts = len(pads)
    rows, heads = refs[:parts], refs[parts : parts + 2]
    before = refs[parts + 2 : parts + 2 + earlier]
    out_ref, acc = refs[parts + 2 + earlier :]
    vocab, width = heads[0].shape
    tokens = acc.shape[1]

    def joined(first, last):
        pieces = []
        for ref, pad in zip(rows, pads):
            pieces.append(ref[:, first:last])
            if pad:
                pieces.append(jnp.zeros((pad, last - first), jnp.bfloat16))
        return jnp.concatenate(pieces, axis=0)

    block = joined(0, width)
    for i, head in enumerate(heads):
        acc[pl.ds(i * vocab, vocab), :] = lax.dot_general(
            head[...], block, NT, preferred_element_type=jnp.float32
        )
    columns = joined(width, width + LANES)
    lane = lax.broadcasted_iota(jnp.int32, (8, LANES), 1)
    weight = jnp.where(lane == 0, 65536.0, jnp.where(lane == 1, 256.0, jnp.where(lane == 2, 1.0, 0.0)))
    ids = lax.dot_general(weight.astype(jnp.bfloat16), columns, NT, preferred_element_type=jnp.float32)
    ids = ids[0:1].astype(jnp.int32)
    z, c = lax.axis_index("z"), lax.axis_index("c")
    place = lax.axis_index("y") * NX + lax.axis_index("x")
    peak = jnp.max(acc[...], axis=0, keepdims=True)
    total = jnp.zeros((1, tokens), jnp.float32)
    target = jnp.zeros((1, tokens), jnp.float32)
    chunk = LANES
    for i in range(2):
        core = c if i == 0 else NC - 1 - c
        local = ids - ((z * NC + core) * TP + place) * vocab

        def add(j, sums):
            logits = acc[pl.ds(pl.multiple_of(i * vocab + j * chunk, chunk), chunk), :]
            entry = lax.broadcasted_iota(jnp.int32, logits.shape, 0) + j * chunk
            return (
                sums[0] + jnp.sum(jnp.exp(logits - peak), axis=0, keepdims=True),
                sums[1] + jnp.sum(jnp.where(entry == local, logits, 0.0), axis=0, keepdims=True),
            )

        total, target = lax.fori_loop(0, vocab // chunk, add, (total, target))
    stats = jnp.concatenate([peak + jnp.log(total), target], axis=0)
    if not earlier:
        out_ref[...] = stats
        return
    own, after, back, near, last = (b[...] for b in before)
    groups = (own, after, stats, back)
    place_y = lax.broadcasted_iota(jnp.int32, (2, LANES), 1) // 32
    place_x = lax.broadcasted_iota(jnp.int32, (2, LANES), 1) % 32 // 8
    docs = {0: near[:, :LANES], 1: near[:, LANES:], NZ - 1: last}
    for i, dz in enumerate(DOCS_A + DOCS_B):
        value = jnp.zeros((2, LANES), jnp.float32)
        for ky in range(NY):
            for kx in range(NX):
                if dz in DOCS_A:
                    source, side = groups[kx][:, :LANES], ky * len(DOCS_A) * 8 + i * 8
                else:
                    source, side = groups[ky][:, LANES:], kx * len(DOCS_B) * 8 + (i - len(DOCS_A)) * 8
                turn = (ky * 32 + kx * 8 - side) % LANES
                moved = pltpu.roll(source, turn, 1) if turn else source
                value = jnp.where(jnp.logical_and(place_y == ky, place_x == kx), moved, value)
        docs[dz] = value
    for dz, value in docs.items():
        out_ref[lax.rem(z + dz, NZ)] = value


def in_vmem(array):
    return pltpu.with_memory_space_constraint(array, VMEM)


def score_group(parts, heads, earlier=(), pads=None):
    vocab, width = heads[0].shape
    pads = pads or (0,) * len(parts)
    tokens = sum(p.shape[0] for p in parts) + sum(pads)
    shape = (NZ, 2, LANES) if earlier else (2, tokens)
    operands = [*map(in_vmem, parts), *heads, *earlier]
    return pl.pallas_call(
        functools.partial(score_kernel, pads, len(earlier)),
        out_shape=jax.ShapeDtypeStruct(shape, jnp.float32),
        in_specs=[pl.BlockSpec(memory_space=VMEM)] * len(operands),
        out_specs=pl.BlockSpec(memory_space=VMEM),
        scratch_shapes=[VMEM((2 * vocab, tokens), jnp.float32)],
        compiler_params=PARAMS,
        cost_estimate=pl.CostEstimate(
            flops=4 * vocab * tokens * width,
            bytes_accessed=(2 * vocab + tokens) * width * 2,
            transcendentals=2 * vocab * tokens,
        ),
        name="score_group",
    )(*operands)


def merged(ref):
    count = ref.shape[0]
    peak = ref[0, 0:1]
    for i in range(1, count):
        peak = jnp.maximum(peak, ref[i, 0:1])
    total = jnp.exp(ref[0, 0:1] - peak)
    target = ref[0, 1:2]
    for i in range(1, count):
        total += jnp.exp(ref[i, 0:1] - peak)
        target += ref[i, 1:2]
    return peak + jnp.log(total), target


def merge_kernel(in_ref, out_ref):
    log_total, target = merged(in_ref)
    value = jnp.concatenate([log_total, target], axis=0)
    outer, inner = lax.axis_index("y"), lax.axis_index("x")
    lane = lax.broadcasted_iota(jnp.int32, value.shape, 1) % 32
    value = pltpu.roll(value, outer * 32, 1)
    value = jnp.where(
        lane >= inner * 8,
        pltpu.roll(value, inner * 8, 1),
        pltpu.roll(value, lax.rem(inner * 8 + 96, 128), 1),
    )
    for i in range(out_ref.shape[0]):
        out_ref[i] = value


def merge_docs(mine):
    return pl.pallas_call(
        merge_kernel,
        out_shape=jax.ShapeDtypeStruct((TP, 2, LANES), jnp.float32),
        in_specs=[pl.BlockSpec(memory_space=VMEM)],
        out_specs=pl.BlockSpec(memory_space=VMEM),
        compiler_params=PARAMS,
        name="merge_docs",
    )(in_vmem(mine))


def final_kernel(length, slots, counts_ref, in_ref, hyp_ref, post_ref):
    log_total, target = merged(in_ref)
    logp = target - log_total
    score = logp
    for k in range(1, length):
        score = score + pltpu.roll(logp, LANES - k, 1)
    score = score / length
    lane = lax.broadcasted_iota(jnp.int32, score.shape, 1)
    head = lane % length == 0
    alive = lane // length < counts_ref[0]
    live = jnp.logical_and(head, alive)
    best = jnp.max(jnp.where(live, score, -jnp.inf), axis=1, keepdims=True)
    total = jnp.sum(jnp.where(live, jnp.exp(jnp.where(live, score - best, 0.0)), 0.0), axis=1, keepdims=True)
    doc_norm = best + jnp.log(total)
    own = (lax.axis_index("y") * NX + lax.axis_index("x")) * slots * length
    turn = lax.rem(LANES - own, LANES)
    for value, ref in ((score, hyp_ref), (score - doc_norm, post_ref)):
        value = jnp.where(alive, value, 0.0)
        value = pltpu.roll(value, turn, 1)
        value = jnp.where(lane == 0, value, pltpu.roll(value, LANES - length + 1, 1))
        ref[...] = value[:, :slots]


def final_scores(whole, doc_counts, length, slots):
    out = jax.ShapeDtypeStruct((1, slots), jnp.float32)
    return pl.pallas_call(
        functools.partial(final_kernel, length, slots),
        out_shape=(out, out),
        in_specs=[pl.BlockSpec(memory_space=SMEM), pl.BlockSpec(memory_space=VMEM)],
        out_specs=(pl.BlockSpec(memory_space=VMEM), pl.BlockSpec(memory_space=VMEM)),
        compiler_params=PARAMS,
        name="final_scores",
    )(doc_counts, in_vmem(whole))


def fetched(block, axis, step):
    count = lax.axis_size(axis)
    return lax.ppermute(block, axis, [((i + step) % count, i) for i in range(count)])


def body(hidden, norm_gain, lm_head, token_ids, doc_counts):
    slots, length = hidden.shape[1], hidden.shape[2]
    heads = (in_vmem(lm_head), in_vmem(fetched(lm_head, "c", 1)))
    payload = norm_rows(hidden, norm_gain, token_ids)
    wide = payload.shape[-1]

    def gathered(block, axis):
        return [block] + [fetched(block, axis, k) for k in range(1, 4)]

    planes = {dz: fetched(payload, "z", dz) for dz in DOCS_A + DOCS_B}
    row = jnp.stack(gathered(payload, "x"))
    plane = jnp.stack(gathered(row, "y"))
    plane_after, plane_before = fetched(plane, "z", 1), fetched(plane, "z", NZ - 1)

    pieces_a = gathered(jnp.stack([planes[dz] for dz in DOCS_A]), "y")
    pieces_b = gathered(jnp.stack([planes[dz] for dz in DOCS_B]), "x")
    low_a, high_a = jnp.stack(pieces_a[:2]), jnp.stack(pieces_a[2:])
    low_b, high_b = jnp.stack(pieces_b[:2]), jnp.stack(pieces_b[2:])

    def flat(*blocks):
        return tuple(b.reshape(-1, wide) for b in blocks)

    pads = (0, LANES - 32 * len(DOCS_A), 0, LANES - 32 * len(DOCS_B))
    relayed = (fetched(low_a, "x", 1), fetched(low_b, "y", 1), fetched(high_a, "x", 3), fetched(high_b, "y", 3))
    kept = (fetched(high_a, "x", 1), fetched(high_b, "y", 1), fetched(low_a, "x", 3), fetched(low_b, "y", 3))
    own = score_group(flat(low_a, high_a, low_b, high_b), heads, pads=pads)
    relayed, own = lax.optimization_barrier((relayed, own))
    far = (
        fetched(relayed[0], "x", 1),
        fetched(relayed[2], "x", 3),
        fetched(relayed[1], "y", 1),
        fetched(relayed[3], "y", 3),
    )
    near = score_group(flat(plane, plane_after), heads)
    last = score_group(flat(plane_before), heads)
    after = score_group(flat(relayed[0], kept[0], relayed[1], kept[1]), heads, pads=pads)
    back = score_group(flat(kept[2], relayed[2], kept[3], relayed[3]), heads, pads=pads)
    sent = score_group(flat(*far), heads, (own, after, back, near, last), pads)
    mine = lax.all_to_all(sent, "z", 0, 0, tiled=True)
    whole = lax.all_to_all(merge_docs(mine), ("y", "x"), 0, 0, tiled=True)
    return final_scores(whole, doc_counts, length, slots)


def solution(mesh):
    fine = Mesh(mesh.devices.reshape(NZ, NC, NY, NX), ("z", "c", "y", "x"))
    docs, slots = ("z", "c"), ("y", "x")
    return jax.shard_map(
        body,
        mesh=fine,
        in_specs=(
            P(docs, slots, None, None),
            P(),
            P(("z", "c", "y", "x"), None),
            P(docs, None, None),
            P(docs),
        ),
        out_specs=(P(docs, slots), P(docs, slots)),
        check_vma=False,
    )
```
